1024 devices in a mesh: blk: 32 (over x_lo, y, core), head: 32 (over x_hi, z).
Axes of the slice: x: 4 (x_hi: 2, x_lo: 2; x = x_hi * 2 + x_lo), y: 8, z: 16, core: 2. Of those that a mesh axis runs over, the one named last changes fastest.
Arguments:
- queries: bfloat16 [131072, 4096], P(('blk', 'head')), may hold values from -128 to 128
- keys: bfloat16 [131072, 1024], P(('blk', 'head')), may hold values from -6 to 6
- values: bfloat16 [131072, 1024], P(('blk', 'head')), may hold values from -9 to 9
- segments: int32 [131072], replicated, may hold values from 0 to 63, never falling along the last dimension, each value on 1 to 8192 neighbouring positions
- norm_gain: float32 [4096], P('head'), may hold values from 0.1 to 1.9
Outputs:
- normed: bfloat16 [131072, 4096], P('blk', 'head')
The draws below stay inside these ranges and needn't reach their ends.
All inputs are finite; a program needn't handle non-finite values.
Results may differ from the reference program's by a relative error of at most 0.012.
Values may be sent and summed in bfloat16 or wider, within the bound.
A program may use at most 32 MiB of HBM per device.

```python
import math
import jax
import jax.numpy as jnp
import numpy as np
from jax import lax

HD = 128
HEADS = 32
KV_HEADS = 8
D = 4096
WINDOW = 512
BLK_TOK = 4096
TOKENS = 131072
N_BLK = 32


def base_keys(key):
    raw_draw = jax.random.normal(jax.random.fold_in(key, 7), (TOKENS, KV_HEADS * HD), jnp.float32)
    return jnp.clip(raw_draw, -6.0, 6.0)


def draw_keys(key, part):
    return base_keys(key).astype(jnp.bfloat16)


def draw_queries(key, part):
    raw_draw = jax.random.normal(jax.random.fold_in(key, 3), (TOKENS, HEADS * HD), jnp.float32)
    raw_draw = jnp.clip(raw_draw, -6.0, 6.0)
    return raw_draw.astype(jnp.bfloat16)


def draw_values(key, part):
    col_head = (jnp.arange(KV_HEADS * HD, dtype=jnp.int32) // HD).astype(jnp.float32)
    frac = col_head / (KV_HEADS - 1)
    raw_draw = jnp.clip(jax.random.normal(jax.random.fold_in(key, 13), (TOKENS, KV_HEADS * HD), jnp.float32), -6.0, 6.0)
    scale = 0.5 * jnp.exp(frac * 1.0986)
    return (raw_draw * scale[None, :]).astype(jnp.bfloat16)


def length_profile(amount, total, bound, skew):
    loads = [(1 << 20) // math.isqrt(grade ** skew) + 1 for grade in range(2, amount + 1)]
    surplus, given = total - bound - (amount - 1), [1] * (amount - 1)
    while surplus > 0:
        free = [i for i in range(amount - 1) if given[i] < bound]
        whole, left = sum([loads[i] for i in free]), surplus
        for i in free:
            addition = min(bound - given[i], max(1, left * loads[i] // whole), surplus)
            given[i] = given[i] + addition
            surplus = surplus - addition
    return np.array([bound] + given)


def ragged(stream_key, amount, total, most, slope):
    if amount == 2:
        one = jax.random.randint(stream_key, (), max(1, total - most), min(most, total - 1) + 1)
        return jnp.stack([one, total - one])
    sizes = jnp.asarray(length_profile(amount, total, most, slope), jnp.int32)
    twos = (amount - 1) // 2
    giver, taker = sizes[1:1 + 2 * twos:2], sizes[2:2 + 2 * twos:2]
    room = jnp.minimum(giver - 1, most - taker)
    moved = jax.random.randint(jax.random.fold_in(stream_key, 1), (twos,), 0, 1 << 20) % (room + 1)
    sizes = sizes.at[1:1 + 2 * twos:2].set(giver - moved).at[2:2 + 2 * twos:2].set(taker + moved)
    return sizes[jax.random.permutation(jax.random.fold_in(stream_key, 2), amount)]


def setup_inputs(seed: int = 0) -> dict:
    key_list = jax.random.split(jax.random.key(seed), 6)
    return {
        "queries": draw_queries(jax.random.fold_in(key_list[5], 71), 0),
        "keys": draw_keys(jax.random.fold_in(key_list[5], 71), 0),
        "values": draw_values(jax.random.fold_in(key_list[5], 71), 0),
        "segments": jnp.searchsorted(jnp.cumsum(ragged(key_list[3], 2 * N_BLK, TOKENS, 2 * BLK_TOK, 2)), jnp.arange(TOKENS), side="right").astype(jnp.int32),
        "norm_gain": jnp.clip(1.0 + 0.18 * jax.random.normal(key_list[4], (D,), jnp.float32), 0.1, 1.9),
    }


def reference(queries, keys, values, segments, norm_gain):
    group_size = HEADS // KV_HEADS
    score_scale = HD ** (-0.5)
    tile = min(512, BLK_TOK)
    span = WINDOW + tile
    pad_keys = jnp.concatenate([jnp.zeros((WINDOW, KV_HEADS * HD), jnp.bfloat16), keys], axis=0)
    pad_values = jnp.concatenate([jnp.zeros((WINDOW, KV_HEADS * HD), jnp.bfloat16), values], axis=0)
    pad_segments = jnp.concatenate([jnp.full((WINDOW,), -1, jnp.int32), segments.astype(jnp.int32)], axis=0)
    rows_here = jnp.arange(tile, dtype=jnp.int32)[:, None]
    cols_here = jnp.arange(span, dtype=jnp.int32)[None, :]
    inside = (cols_here > rows_here) & (cols_here <= rows_here + WINDOW)

    def one_tile(index):
        start = (index * tile).astype(jnp.int32)
        query_tile = lax.dynamic_slice_in_dim(queries, start, tile, 0).astype(jnp.float32).reshape(tile, KV_HEADS, group_size, HD)
        key_tile = lax.dynamic_slice_in_dim(pad_keys, start, span, 0).astype(jnp.float32).reshape(span, KV_HEADS, HD)
        value_tile = lax.dynamic_slice_in_dim(pad_values, start, span, 0).astype(jnp.float32).reshape(span, KV_HEADS, HD)
        query_seg = lax.dynamic_slice_in_dim(segments.astype(jnp.int32), start, tile, 0)
        key_seg = lax.dynamic_slice_in_dim(pad_segments, start, span, 0)
        allowed = inside & (key_seg[None, :] == query_seg[:, None])
        scores = jnp.einsum('qcgd,kcd->cgqk', query_tile, key_tile) * score_scale
        rowmax = lax.optimization_barrier(jnp.max(jnp.where(allowed, scores, -1e+30), axis=3, keepdims=True))
        prob = jnp.where(allowed, jnp.exp(scores - rowmax), 0.0)
        total = lax.optimization_barrier(jnp.sum(prob, axis=3, keepdims=True))
        weights = prob.astype(jnp.bfloat16).astype(jnp.float32)
        weighted = jnp.einsum('cgqk,kcd->cgqd', weights, value_tile) / total
        return jnp.transpose(weighted, (2, 0, 1, 3)).reshape(tile, D).astype(jnp.bfloat16)
    tiles = lax.map(one_tile, jnp.arange(TOKENS // tile, dtype=jnp.int32))
    attn = tiles.reshape(TOKENS, D)
    wide = attn.astype(jnp.float32)
    squares = lax.optimization_barrier(jnp.sum(wide * wide, axis=1, keepdims=True))
    normed = (wide * norm_gain[None, :] / jnp.sqrt(squares / D + 1e-05)).astype(jnp.bfloat16)
    return normed
```

```python
import functools
import math

import jax
import jax.numpy as jnp
from jax import lax
from jax.experimental import pallas as pl
from jax.experimental.pallas import tpu as pltpu
from jax.sharding import PartitionSpec as P

HD = 128
HEADS = 32
KV_HEADS = 8
WINDOW = 512
EPS = 1e-05
MESH = pl.DeviceIdType.MESH


def kernel(
    nb, nh, chunk, halo, kv_heads, group,
    q_ref, k_ref, v_ref, seg_ref, o_ref,
    kext, vext, qbuf, segbuf, bias, attn, obuf, squares,
    plus_send, plus_recv, minus_send, minus_recv, own_sem, seg_sem, o_send, o_recv,
):
    b = lax.axis_index("blk")
    h = lax.axis_index("head")
    total_ranks = nb * nh
    rank = b * nh + h
    nxt = lax.rem(rank + 1, total_ranks)
    prv = lax.rem(rank + total_ranks - 1, total_ranks)
    nxt_b, nxt_h = lax.div(nxt, nh), lax.rem(nxt, nh)
    nxt_id = (nxt_b, nxt_h)
    prv_id = (lax.div(prv, nh), lax.rem(prv, nh))
    before_b = lax.rem(b + nb - 1, nb)

    own_rows = pl.ds((halo - 1) * chunk, chunk)
    own_k = pltpu.make_async_copy(k_ref, kext.at[own_rows, :], own_sem.at[0])
    own_v = pltpu.make_async_copy(v_ref, vext.at[own_rows, :], own_sem.at[1])
    own_k.start()
    own_v.start()

    def seg_copy(m):
        row = jnp.maximum(nxt - halo + m, 0)
        return pltpu.make_async_copy(seg_ref.at[row], segbuf.at[m], seg_sem.at[m])

    for m in range(halo + 1):
        seg_copy(m).start()

    barrier = pltpu.get_barrier_semaphore()

    def greet(g, carry):
        @pl.when(g != h)
        def _():
            pl.semaphore_signal(barrier, inc=1, device_id=(b, g), device_id_type=MESH)

        return carry

    lax.fori_loop(0, nh - 1, greet, 0)
    pl.semaphore_signal(barrier, inc=1, device_id=(before_b, nh - 1), device_id_type=MESH)

    @pl.when(h >= nh - 2)
    def _():
        pl.semaphore_signal(barrier, inc=1, device_id=nxt_id, device_id_type=MESH)

    extra = jnp.where(h == 0, 1, 0) + jnp.where(h == nh - 1, 2, 0)
    pl.semaphore_wait(barrier, nh - 1 + extra)

    def cols(c, width):
        return pl.ds(pl.multiple_of(c * width, width), width)

    def plus_copy(hop, tensor, c):
        ext, own = (kext, k_ref) if tensor == 0 else (vext, v_ref)
        lanes = cols(c, HD)
        target = ext.at[pl.ds((halo - 2 - hop) * chunk, chunk), lanes]
        if hop == 0:
            source = own.at[:, lanes]
        else:
            source = ext.at[pl.ds((halo - 1 - hop) * chunk, chunk), lanes]
        return pltpu.make_async_remote_copy(
            src_ref=source, dst_ref=target,
            send_sem=plus_send.at[hop, tensor], recv_sem=plus_recv.at[hop, tensor, c],
            device_id=nxt_id, device_id_type=MESH,
        )

    def minus_copy(tensor, c):
        if tensor == 2:
            lanes = cols(c, group * HD)
            source, target = q_ref.at[:, lanes], qbuf.at[:, lanes]
        else:
            ext, own = (kext, k_ref) if tensor == 0 else (vext, v_ref)
            lanes = cols(c, HD)
            source, target = own.at[:, lanes], ext.at[pl.ds(halo * chunk, chunk), lanes]
        return pltpu.make_async_remote_copy(
            src_ref=source, dst_ref=target,
            send_sem=minus_send.at[tensor], recv_sem=minus_recv.at[tensor, c],
            device_id=prv_id, device_id_type=MESH,
        )

    def start_first(c, carry):
        for tensor in range(2):
            plus_copy(0, tensor, c).start()
        for tensor in range(3):
            minus_copy(tensor, c).start()
        return carry

    lax.fori_loop(0, kv_heads, start_first, 0)

    for m in range(halo + 1):
        seg_copy(m).wait()
    row_pos = lax.broadcasted_iota(jnp.int32, (chunk, chunk), 0)
    col_pos = lax.broadcasted_iota(jnp.int32, (chunk, chunk), 1)
    query_seg = jnp.transpose(jnp.broadcast_to(segbuf[halo], (chunk, chunk)))
    for m in range(halo + 1):
        key_seg = jnp.broadcast_to(segbuf[m], (chunk, chunk))
        col = col_pos + m * chunk
        allowed = (col > row_pos) & (col <= row_pos + WINDOW) & (key_seg == query_seg)
        allowed = allowed & ((nxt - halo + m) * chunk + col_pos >= 0)
        bias[:, m * chunk : (m + 1) * chunk] = jnp.where(allowed, 0.0, -1e30)

    for hop in range(1, halo - 1):

        def forward(c, carry):
            for tensor in range(2):
                plus_copy(hop - 1, tensor, c).wait_recv()
                plus_copy(hop, tensor, c).start()
            return carry

        lax.fori_loop(0, kv_heads, forward, 0)

    own_k.wait()
    own_v.wait()
    squares[...] = jnp.zeros_like(squares)
    to_exponent = HD ** (-0.5) * math.log2(math.e)
    span = (halo + 1) * chunk

    def attend(c, carry):
        for tensor in range(2):
            plus_copy(halo - 2, tensor, c).wait_recv()
        for tensor in range(3):
            minus_copy(tensor, c).wait_recv()
        key = kext[:, cols(c, HD)]
        value = vext[:, cols(c, HD)]
        query = jnp.concatenate(
            [qbuf[:, cols(c * group + u, HD)] for u in range(group)], axis=0
        )
        scores = lax.dot_general(
            query, key, (((1,), (1,)), ((), ())), preferred_element_type=jnp.float32
        )
        scores = scores.reshape(group, chunk, span) + bias[...][None]
        rowmax = jnp.max(scores, axis=2, keepdims=True)
        prob = jnp.exp2((scores - rowmax) * to_exponent)
        total = jnp.sum(prob, axis=2, keepdims=True)
        weighted = jnp.dot(
            prob.astype(jnp.bfloat16).reshape(group * chunk, span), value,
            preferred_element_type=jnp.float32,
        )
        out = weighted.reshape(group, chunk, HD) / total
        attn[pl.ds(c * group, group)] = out
        squares[...] += jnp.sum(out * out, axis=0)
        return carry

    lax.fori_loop(0, kv_heads, attend, 0)

    width = nh * HD
    inv = lax.rsqrt(jnp.sum(squares[...], axis=1, keepdims=True) / width + EPS)
    out_rows = pl.ds(pl.multiple_of(nxt_h * chunk, chunk), chunk)

    def spread(j, carry):
        g = lax.rem(h + 1 + j, nh)
        obuf[g] = (attn[g] * inv).astype(jnp.bfloat16)
        stays = (nxt_b == b) & (g == h)

        @pl.when(stays)
        def _():
            pltpu.make_async_copy(obuf.at[g], o_ref.at[out_rows, :], o_recv).start()

        @pl.when(jnp.logical_not(stays))
        def _():
            pltpu.make_async_remote_copy(
                src_ref=obuf.at[g], dst_ref=o_ref.at[out_rows, :],
                send_sem=o_send, recv_sem=o_recv,
                device_id=(nxt_b, g), device_id_type=MESH,
            ).start()

        return carry

    lax.fori_loop(0, nh, spread, 0)

    for hop in range(halo - 1):
        for tensor, ext in ((0, kext), (1, vext)):
            rows = ext.at[pl.ds(0, chunk), :]
            pltpu.make_async_copy(rows, rows, plus_send.at[hop, tensor]).wait()
    for tensor, ext in ((0, kext), (1, vext)):
        rows = ext.at[pl.ds(0, chunk), :]
        pltpu.make_async_copy(rows, rows, minus_send.at[tensor]).wait()
    pltpu.make_async_copy(qbuf, qbuf, minus_send.at[2]).wait()

    @pl.when(h == nh - 1)
    def _():
        pltpu.make_async_copy(obuf, obuf, o_send).wait()

    @pl.when(h != nh - 1)
    def _():
        some = obuf.at[pl.ds(0, nh - 1)]
        pltpu.make_async_copy(some, some, o_send).wait()

    pltpu.make_async_copy(o_ref, o_ref, o_recv).wait()


def per_device(queries, keys, values, segments, norm_gain):
    nb, nh = lax.axis_size("blk"), lax.axis_size("head")
    chunk = queries.shape[0]
    halo = WINDOW // chunk
    kv_heads = keys.shape[1] // HD
    group = queries.shape[1] // keys.shape[1]
    any_spec = pl.BlockSpec(memory_space=pl.ANY)
    span = (halo + 1) * chunk
    spread = pl.pallas_call(
        functools.partial(kernel, nb, nh, chunk, halo, kv_heads, group),
        out_shape=jax.ShapeDtypeStruct((nh * chunk, HD), jnp.bfloat16),
        in_specs=[any_spec] * 4,
        out_specs=any_spec,
        scratch_shapes=[
            pltpu.VMEM((span, kv_heads * HD), jnp.bfloat16),
            pltpu.VMEM((span, kv_heads * HD), jnp.bfloat16),
            pltpu.VMEM((chunk, nh * HD), jnp.bfloat16),
            pltpu.VMEM((halo + 1, 1, chunk), jnp.int32),
            pltpu.VMEM((chunk, span), jnp.float32),
            pltpu.VMEM((nh, chunk, HD), jnp.float32),
            pltpu.VMEM((nh, chunk, HD), jnp.bfloat16),
            pltpu.VMEM((chunk, HD), jnp.float32),
            pltpu.SemaphoreType.DMA((halo - 1, 2)),
            pltpu.SemaphoreType.DMA((halo - 1, 2, kv_heads)),
            pltpu.SemaphoreType.DMA((3,)),
            pltpu.SemaphoreType.DMA((3, kv_heads)),
            pltpu.SemaphoreType.DMA((2,)),
            pltpu.SemaphoreType.DMA((halo + 1,)),
            pltpu.SemaphoreType.DMA,
            pltpu.SemaphoreType.DMA,
        ],
        compiler_params=pltpu.CompilerParams(
            collective_id=0, has_side_effects=True, vmem_limit_bytes=40 * 1024 * 1024
        ),
        name="attend_and_spread",
    )(queries, keys, values, segments.reshape(-1, 1, chunk))
    return (spread.astype(jnp.float32) * norm_gain[None, :]).astype(jnp.bfloat16)


def solution(mesh):
    placed = (
        P(("blk", "head"), None),
        P(("blk", "head"), None),
        P(("blk", "head"), None),
        P(),
        P("head"),
    )
    return jax.shard_map(
        per_device, mesh=mesh, in_specs=placed, out_specs=P("blk", "head"), check_vma=False
    )
```

```python
import functools
import math

import jax
import jax.numpy as jnp
from jax import lax
from jax.experimental import pallas as pl
from jax.experimental.pallas import tpu as pltpu
from jax.sharding import PartitionSpec as P

HD = 128
HEADS = 32
KV_HEADS = 8
WINDOW = 512
EPS = 1e-05
MESH = pl.DeviceIdType.MESH


def kernel(
    nb, nh, chunk, halo, kv_heads, group,
    q_ref, k_ref, v_ref, seg_ref, o_ref,
    kext, vext, qbuf, segbuf, bias, attn, obuf, squares,
    plus_send, plus_recv, minus_send, minus_recv, own_sem, seg_sem, o_send, o_recv,
    rounds_sem,
):
    b = lax.axis_index("blk")
    h = lax.axis_index("head")
    total_ranks = nb * nh
    rank = b * nh + h
    nxt = lax.rem(rank + 1, total_ranks)
    prv = lax.rem(rank + total_ranks - 1, total_ranks)
    nxt_b, nxt_h = lax.div(nxt, nh), lax.rem(nxt, nh)
    nxt_id = (nxt_b, nxt_h)
    prv_id = (lax.div(prv, nh), lax.rem(prv, nh))

    own_rows = pl.ds((halo - 1) * chunk, chunk)
    own_k = pltpu.make_async_copy(k_ref, kext.at[own_rows, :], own_sem.at[0])
    own_v = pltpu.make_async_copy(v_ref, vext.at[own_rows, :], own_sem.at[1])
    own_k.start()
    own_v.start()

    def seg_copy(m):
        row = jnp.maximum(nxt - halo + m, 0)
        return pltpu.make_async_copy(seg_ref.at[row], segbuf.at[m], seg_sem.at[m])

    for m in range(halo + 1):
        seg_copy(m).start()

    def rank_id(r):
        return (lax.div(r, nh), lax.rem(r, nh))

    def signal_both(sem, distance):
        for r in (rank + distance, rank + total_ranks - distance):
            pl.semaphore_signal(
                sem, inc=1, device_id=rank_id(lax.rem(r, total_ranks)), device_id_type=MESH
            )

    barrier = pltpu.get_barrier_semaphore()
    signal_both(barrier, 1)
    pl.semaphore_wait(barrier, 2)
    rounds = nh.bit_length() - 1
    signal_both(rounds_sem.at[0], 1)

    def meet(j):
        pl.semaphore_wait(rounds_sem.at[j], 2)
        if j + 1 < rounds:
            signal_both(rounds_sem.at[j + 1], 2 << j)

    def cols(c, width):
        return pl.ds(pl.multiple_of(c * width, width), width)

    def plus_copy(hop, tensor, c):
        ext, own = (kext, k_ref) if tensor == 0 else (vext, v_ref)
        lanes = cols(c, HD)
        target = ext.at[pl.ds((halo - 2 - hop) * chunk, chunk), lanes]
        if hop == 0:
            source = own.at[:, lanes]
        else:
            source = ext.at[pl.ds((halo - 1 - hop) * chunk, chunk), lanes]
        return pltpu.make_async_remote_copy(
            src_ref=source, dst_ref=target,
            send_sem=plus_send.at[hop, tensor], recv_sem=plus_recv.at[hop, tensor, c],
            device_id=nxt_id, device_id_type=MESH,
        )

    def minus_copy(tensor, c):
        if tensor == 2:
            lanes = cols(c, group * HD)
            source, target = q_ref.at[:, lanes], qbuf.at[:, lanes]
        else:
            ext, own = (kext, k_ref) if tensor == 0 else (vext, v_ref)
            lanes = cols(c, HD)
            source, target = own.at[:, lanes], ext.at[pl.ds(halo * chunk, chunk), lanes]
        return pltpu.make_async_remote_copy(
            src_ref=source, dst_ref=target,
            send_sem=minus_send.at[tensor], recv_sem=minus_recv.at[tensor, c],
            device_id=prv_id, device_id_type=MESH,
        )

    def start_first(c, carry):
        for tensor in range(2):
            plus_copy(0, tensor, c).start()
        for tensor in range(3):
            minus_copy(tensor, c).start()
        return carry

    lax.fori_loop(0, kv_heads, start_first, 0)

    for m in range(halo + 1):
        seg_copy(m).wait()
    row_pos = lax.broadcasted_iota(jnp.int32, (chunk, chunk), 0)
    col_pos = lax.broadcasted_iota(jnp.int32, (chunk, chunk), 1)
    query_seg = jnp.transpose(jnp.broadcast_to(segbuf[halo], (chunk, chunk)))
    for m in range(halo + 1):
        key_seg = jnp.broadcast_to(segbuf[m], (chunk, chunk))
        col = col_pos + m * chunk
        allowed = (col > row_pos) & (col <= row_pos + WINDOW) & (key_seg == query_seg)
        allowed = allowed & ((nxt - halo + m) * chunk + col_pos >= 0)
        bias[:, m * chunk : (m + 1) * chunk] = jnp.where(allowed, 0.0, -1e30)

    meet(0)
    for hop in range(1, halo - 1):

        def forward(c, carry):
            for tensor in range(2):
                plus_copy(hop - 1, tensor, c).wait_recv()
                plus_copy(hop, tensor, c).start()
            return carry

        lax.fori_loop(0, kv_heads, forward, 0)
        if hop < rounds:
            meet(hop)

    own_k.wait()
    own_v.wait()
    squares[...] = jnp.zeros_like(squares)
    to_exponent = HD ** (-0.5) * math.log2(math.e)
    span = (halo + 1) * chunk

    def attend(c, carry):
        for j in range(halo - 1, rounds):

            @pl.when(c == (j - 2) * kv_heads // 3)
            def _():
                meet(j)

        for tensor in range(2):
            plus_copy(halo - 2, tensor, c).wait_recv()
        for tensor in range(3):
            minus_copy(tensor, c).wait_recv()
        key = kext[:, cols(c, HD)]
        value = vext[:, cols(c, HD)]
        query = jnp.concatenate(
            [qbuf[:, cols(c * group + u, HD)] for u in range(group)], axis=0
        )
        scores = lax.dot_general(
            query, key, (((1,), (1,)), ((), ())), preferred_element_type=jnp.float32
        )
        scores = scores.reshape(group, chunk, span) + bias[...][None]
        rowmax = jnp.max(scores, axis=2, keepdims=True)
        prob = jnp.exp2((scores - rowmax) * to_exponent)
        total = jnp.sum(prob, axis=2, keepdims=True)
        weighted = jnp.dot(
            prob.astype(jnp.bfloat16).reshape(group * chunk, span), value,
            preferred_element_type=jnp.float32,
        )
        out = weighted.reshape(group, chunk, HD) / total
        attn[pl.ds(c * group, group)] = out
        squares[...] += jnp.sum(out * out, axis=0)
        return carry

    lax.fori_loop(0, kv_heads, attend, 0)

    width = nh * HD
    inv = lax.rsqrt(jnp.sum(squares[...], axis=1, keepdims=True) / width + EPS)
    out_rows = pl.ds(pl.multiple_of(nxt_h * chunk, chunk), chunk)

    def spread(j, carry):
        g = lax.rem(h + 1 + j, nh)
        obuf[g] = (attn[g] * inv).astype(jnp.bfloat16)
        stays = (nxt_b == b) & (g == h)

        @pl.when(stays)
        def _():
            pltpu.make_async_copy(obuf.at[g], o_ref.at[out_rows, :], o_recv).start()

        @pl.when(jnp.logical_not(stays))
        def _():
            pltpu.make_async_remote_copy(
                src_ref=obuf.at[g], dst_ref=o_ref.at[out_rows, :],
                send_sem=o_send, recv_sem=o_recv,
                device_id=(nxt_b, g), device_id_type=MESH,
            ).start()

        return carry

    lax.fori_loop(0, nh, spread, 0)

    for hop in range(halo - 1):
        for tensor, ext in ((0, kext), (1, vext)):
            rows = ext.at[pl.ds(0, chunk), :]
            pltpu.make_async_copy(rows, rows, plus_send.at[hop, tensor]).wait()
    for tensor, ext in ((0, kext), (1, vext)):
        rows = ext.at[pl.ds(0, chunk), :]
        pltpu.make_async_copy(rows, rows, minus_send.at[tensor]).wait()
    pltpu.make_async_copy(qbuf, qbuf, minus_send.at[2]).wait()

    @pl.when(h == nh - 1)
    def _():
        pltpu.make_async_copy(obuf, obuf, o_send).wait()

    @pl.when(h != nh - 1)
    def _():
        some = obuf.at[pl.ds(0, nh - 1)]
        pltpu.make_async_copy(some, some, o_send).wait()

    pltpu.make_async_copy(o_ref, o_ref, o_recv).wait()


def per_device(queries, keys, values, segments, norm_gain):
    nb, nh = lax.axis_size("blk"), lax.axis_size("head")
    chunk = queries.shape[0]
    halo = WINDOW // chunk
    kv_heads = keys.shape[1] // HD
    group = queries.shape[1] // keys.shape[1]
    any_spec = pl.BlockSpec(memory_space=pl.ANY)
    span = (halo + 1) * chunk
    spread = pl.pallas_call(
        functools.partial(kernel, nb, nh, chunk, halo, kv_heads, group),
        out_shape=jax.ShapeDtypeStruct((nh * chunk, HD), jnp.bfloat16),
        in_specs=[any_spec] * 4,
        out_specs=any_spec,
        scratch_shapes=[
            pltpu.VMEM((span, kv_heads * HD), jnp.bfloat16),
            pltpu.VMEM((span, kv_heads * HD), jnp.bfloat16),
            pltpu.VMEM((chunk, nh * HD), jnp.bfloat16),
            pltpu.VMEM((halo + 1, 1, chunk), jnp.int32),
            pltpu.VMEM((chunk, span), jnp.float32),
            pltpu.VMEM((nh, chunk, HD), jnp.float32),
            pltpu.VMEM((nh, chunk, HD), jnp.bfloat16),
            pltpu.VMEM((chunk, HD), jnp.float32),
            pltpu.SemaphoreType.DMA((halo - 1, 2)),
            pltpu.SemaphoreType.DMA((halo - 1, 2, kv_heads)),
            pltpu.SemaphoreType.DMA((3,)),
            pltpu.SemaphoreType.DMA((3, kv_heads)),
            pltpu.SemaphoreType.DMA((2,)),
            pltpu.SemaphoreType.DMA((halo + 1,)),
            pltpu.SemaphoreType.DMA,
            pltpu.SemaphoreType.DMA,
            pltpu.SemaphoreType.REGULAR((nh.bit_length() - 1,)),
        ],
        compiler_params=pltpu.CompilerParams(
            collective_id=0, has_side_effects=True, vmem_limit_bytes=62 * 1024 * 1024
        ),
        name="attend_and_spread",
    )(queries, keys, values, segments.reshape(-1, 1, chunk))
    return (spread.astype(jnp.float32) * norm_gain[None, :]).astype(jnp.bfloat16)


def solution(mesh):
    placed = (
        P(("blk", "head"), None),
        P(("blk", "head"), None),
        P(("blk", "head"), None),
        P(),
        P("head"),
    )
    return jax.shard_map(
        per_device, mesh=mesh, in_specs=placed, out_specs=P("blk", "head"), check_vma=False
    )
```

```python
import functools
import math

import jax
import jax.numpy as jnp
from jax import lax
from jax.experimental import pallas as pl
from jax.experimental.pallas import tpu as pltpu
from jax.sharding import PartitionSpec as P

HD = 128
HEADS = 32
KV_HEADS = 8
WINDOW = 512
EPS = 1e-05
ORDER = sum(step << (3 * place) for place, step in enumerate((5, 3, 6, 2, 1, 7, 4, 0)))
MESH = pl.DeviceIdType.MESH


def kernel(
    nb, nh, chunk, halo, kv_heads, group,
    q_ref, k_ref, v_ref, seg_ref, o_ref, i_ref,
    kext, vext, qbuf, segbuf, bias, obuf, squares, inv,
    plus_send, plus_recv, minus_send, minus_recv, own_sem, seg_sem, o_send, o_recv,
    i_send, i_recv, rounds_sem,
):
    b = lax.axis_index("blk")
    h = lax.axis_index("head")
    total_ranks = nb * nh
    rank = b * nh + h
    nxt = lax.rem(rank + 1, total_ranks)
    prv = lax.rem(rank + total_ranks - 1, total_ranks)
    nxt_b, nxt_h = lax.div(nxt, nh), lax.rem(nxt, nh)
    nxt_id = (nxt_b, nxt_h)
    prv_h = lax.rem(prv, nh)
    prv_id = (lax.div(prv, nh), prv_h)

    own_rows = pl.ds((halo - 1) * chunk, chunk)
    own_k = pltpu.make_async_copy(k_ref, kext.at[own_rows, :], own_sem.at[0])
    own_v = pltpu.make_async_copy(v_ref, vext.at[own_rows, :], own_sem.at[1])
    own_k.start()
    own_v.start()

    def seg_copy(m):
        row = jnp.maximum(nxt - halo + m, 0)
        return pltpu.make_async_copy(seg_ref.at[row], segbuf.at[m], seg_sem.at[m])

    for m in range(halo + 1):
        seg_copy(m).start()

    def rank_id(r):
        return (lax.div(r, nh), lax.rem(r, nh))

    def signal_both(sem, distance):
        for r in (rank + distance, rank + total_ranks - distance):
            pl.semaphore_signal(
                sem, inc=1, device_id=rank_id(lax.rem(r, total_ranks)), device_id_type=MESH
            )

    barrier = pltpu.get_barrier_semaphore()
    signal_both(barrier, 1)
    pl.semaphore_wait(barrier, 2)
    rounds = nh.bit_length() - 1
    signal_both(rounds_sem.at[0], 1)

    def meet(j):
        pl.semaphore_wait(rounds_sem.at[j], 2)
        if j + 1 < rounds:
            signal_both(rounds_sem.at[j + 1], 2 << j)

    def pick(code, head):
        quad = lax.div(head, group)
        if kv_heads != 8:
            return lax.rem(quad + code, kv_heads), code + 1
        step = lax.rem(code, 8)
        flip = lax.rem(lax.div(quad, 4) + lax.div(step, 4), 2)
        return flip * 4 + lax.rem(quad + step, 4), lax.div(code, 8)

    start_code = ORDER if kv_heads == 8 else 0

    def cols(c, width):
        return pl.ds(pl.multiple_of(c * width, width), width)

    def plus_copy(hop, tensor, c):
        ext, own = (kext, k_ref) if tensor == 0 else (vext, v_ref)
        lanes = cols(c, HD)
        target = ext.at[pl.ds((halo - 2 - hop) * chunk, chunk), lanes]
        if hop == 0:
            source = own.at[:, lanes]
        else:
            source = ext.at[pl.ds((halo - 1 - hop) * chunk, chunk), lanes]
        return pltpu.make_async_remote_copy(
            src_ref=source, dst_ref=target,
            send_sem=plus_send.at[hop, tensor], recv_sem=plus_recv.at[hop, tensor, c],
            device_id=nxt_id, device_id_type=MESH,
        )

    def minus_copy(tensor, c):
        if tensor == 2:
            lanes = cols(c, group * HD)
            source, target = q_ref.at[:, lanes], qbuf.at[:, lanes]
        else:
            ext, own = (kext, k_ref) if tensor == 0 else (vext, v_ref)
            lanes = cols(c, HD)
            source, target = own.at[:, lanes], ext.at[pl.ds(halo * chunk, chunk), lanes]
        return pltpu.make_async_remote_copy(
            src_ref=source, dst_ref=target,
            send_sem=minus_send.at[tensor], recv_sem=minus_recv.at[tensor, c],
            device_id=prv_id, device_id_type=MESH,
        )

    def start_first(s, code):
        plus_c, _ = pick(code, nxt_h)
        minus_c, code = pick(code, prv_h)
        for tensor in range(2):
            plus_copy(0, tensor, plus_c).start()
        for tensor in range(3):
            minus_copy(tensor, minus_c).start()
        return code

    lax.fori_loop(0, kv_heads, start_first, start_code)

    for m in range(halo + 1):
        seg_copy(m).wait()
    row_pos = lax.broadcasted_iota(jnp.int32, (chunk, chunk), 0)
    col_pos = lax.broadcasted_iota(jnp.int32, (chunk, chunk), 1)
    query_seg = jnp.transpose(jnp.broadcast_to(segbuf[halo], (chunk, chunk)))
    for m in range(halo + 1):
        key_seg = jnp.broadcast_to(segbuf[m], (chunk, chunk))
        col = col_pos + m * chunk
        allowed = (col > row_pos) & (col <= row_pos + WINDOW) & (key_seg == query_seg)
        allowed = allowed & ((nxt - halo + m) * chunk + col_pos >= 0)
        bias[:, m * chunk : (m + 1) * chunk] = jnp.where(allowed, 0.0, -1e30)

    meet(0)
    for hop in range(1, halo - 1):

        def forward(s, code):
            c, code = pick(code, nxt_h)
            for tensor in range(2):
                plus_copy(hop - 1, tensor, c).wait_recv()
                plus_copy(hop, tensor, c).start()
            return code

        lax.fori_loop(0, kv_heads, forward, start_code)
        if hop < rounds:
            meet(hop)

    own_k.wait()
    own_v.wait()
    for j in range(halo - 1, rounds):
        meet(j)
    squares[...] = jnp.zeros_like(squares)
    out_rows = pl.ds(pl.multiple_of(nxt_h * chunk, chunk), chunk)

    def send_head(g):
        stays = (nxt_b == b) & (g == h)

        @pl.when(stays)
        def _():
            pltpu.make_async_copy(obuf.at[g], o_ref.at[out_rows, :], o_recv).start()

        @pl.when(jnp.logical_not(stays))
        def _():
            pltpu.make_async_remote_copy(
                src_ref=obuf.at[g], dst_ref=o_ref.at[out_rows, :],
                send_sem=o_send, recv_sem=o_recv,
                device_id=(nxt_b, g), device_id_type=MESH,
            ).start()

    to_exponent = HD ** (-0.5) * math.log2(math.e)
    span = (halo + 1) * chunk

    def attend(s, code):
        c, code = pick(code, h)
        for tensor in range(2):
            plus_copy(halo - 2, tensor, c).wait_recv()
        for tensor in range(3):
            minus_copy(tensor, c).wait_recv()
        key = kext[:, cols(c, HD)]
        value = vext[:, cols(c, HD)]
        query = jnp.concatenate(
            [qbuf[:, cols(c * group + u, HD)] for u in range(group)], axis=0
        )
        scores = lax.dot_general(
            query, key, (((1,), (1,)), ((), ())), preferred_element_type=jnp.float32
        )
        scores = scores.reshape(group, chunk, span) + bias[...][None]
        rowmax = jnp.max(scores, axis=2, keepdims=True)
        prob = jnp.exp2((scores - rowmax) * to_exponent)
        total = jnp.sum(prob, axis=2, keepdims=True)
        weighted = jnp.dot(
            prob.astype(jnp.bfloat16).reshape(group * chunk, span), value,
            preferred_element_type=jnp.float32,
        )
        out = weighted.reshape(group, chunk, HD) / total
        out = out.astype(jnp.bfloat16)
        obuf[pl.ds(c * group, group)] = out
        wide = out.astype(jnp.float32)
        squares[...] += jnp.sum(wide * wide, axis=0)
        for u in range(group):
            send_head(c * group + u)
        return code

    lax.fori_loop(0, kv_heads, attend, start_code)

    width = nh * HD
    mean = jnp.sum(jnp.transpose(squares[...]), axis=0, keepdims=True) / width
    inv[...] = lax.rsqrt(mean + EPS)

    def send_inv(j, carry):
        g = lax.rem(h + 1 + j, nh)
        stays = (nxt_b == b) & (g == h)

        @pl.when(stays)
        def _():
            pltpu.make_async_copy(inv, i_ref.at[nxt_h], i_recv).start()

        @pl.when(jnp.logical_not(stays))
        def _():
            pltpu.make_async_remote_copy(
                src_ref=inv, dst_ref=i_ref.at[nxt_h], send_sem=i_send, recv_sem=i_recv,
                device_id=(nxt_b, g), device_id_type=MESH,
            ).start()

        return carry

    lax.fori_loop(0, nh, send_inv, 0)

    for hop in range(halo - 1):
        for tensor, ext in ((0, kext), (1, vext)):
            rows = ext.at[pl.ds(0, chunk), :]
            pltpu.make_async_copy(rows, rows, plus_send.at[hop, tensor]).wait()
    for tensor, ext in ((0, kext), (1, vext)):
        rows = ext.at[pl.ds(0, chunk), :]
        pltpu.make_async_copy(rows, rows, minus_send.at[tensor]).wait()
    pltpu.make_async_copy(qbuf, qbuf, minus_send.at[2]).wait()

    @pl.when(h == nh - 1)
    def _():
        pltpu.make_async_copy(obuf, obuf, o_send).wait()
        pltpu.make_async_copy(i_ref, i_ref, i_send).wait()

    @pl.when(h != nh - 1)
    def _():
        some = obuf.at[pl.ds(0, nh - 1)]
        pltpu.make_async_copy(some, some, o_send).wait()
        rows = i_ref.at[pl.ds(0, nh - 1)]
        pltpu.make_async_copy(rows, rows, i_send).wait()

    pltpu.make_async_copy(o_ref, o_ref, o_recv).wait()
    pltpu.make_async_copy(i_ref, i_ref, i_recv).wait()


def per_device(queries, keys, values, segments, norm_gain):
    nb, nh = lax.axis_size("blk"), lax.axis_size("head")
    chunk = queries.shape[0]
    halo = WINDOW // chunk
    kv_heads = keys.shape[1] // HD
    group = queries.shape[1] // keys.shape[1]
    any_spec = pl.BlockSpec(memory_space=pl.ANY)
    span = (halo + 1) * chunk
    attn, inv = pl.pallas_call(
        functools.partial(kernel, nb, nh, chunk, halo, kv_heads, group),
        out_shape=(
            jax.ShapeDtypeStruct((nh * chunk, HD), jnp.bfloat16),
            jax.ShapeDtypeStruct((nh, 1, chunk), jnp.float32),
        ),
        in_specs=[any_spec] * 4,
        out_specs=(any_spec, any_spec),
        scratch_shapes=[
            pltpu.VMEM((span, kv_heads * HD), jnp.bfloat16),
            pltpu.VMEM((span, kv_heads * HD), jnp.bfloat16),
            pltpu.VMEM((chunk, nh * HD), jnp.bfloat16),
            pltpu.VMEM((halo + 1, 1, chunk), jnp.int32),
            pltpu.VMEM((chunk, span), jnp.float32),
            pltpu.VMEM((nh, chunk, HD), jnp.bfloat16),
            pltpu.VMEM((chunk, HD), jnp.float32),
            pltpu.VMEM((1, chunk), jnp.float32),
            pltpu.SemaphoreType.DMA((halo - 1, 2)),
            pltpu.SemaphoreType.DMA((halo - 1, 2, kv_heads)),
            pltpu.SemaphoreType.DMA((3,)),
            pltpu.SemaphoreType.DMA((3, kv_heads)),
            pltpu.SemaphoreType.DMA((2,)),
            pltpu.SemaphoreType.DMA((halo + 1,)),
            pltpu.SemaphoreType.DMA,
            pltpu.SemaphoreType.DMA,
            pltpu.SemaphoreType.DMA,
            pltpu.SemaphoreType.DMA,
            pltpu.SemaphoreType.REGULAR((nh.bit_length() - 1,)),
        ],
        compiler_params=pltpu.CompilerParams(
            collective_id=0, has_side_effects=True, vmem_limit_bytes=62 * 1024 * 1024
        ),
        name="attend_and_spread",
    )(queries, keys, values, segments.reshape(-1, 1, chunk))
    wide = attn.astype(jnp.float32)
    return (wide * norm_gain[None, :] * inv.reshape(-1, 1)).astype(jnp.bfloat16)


def solution(mesh):
    placed = (
        P(("blk", "head"), None),
        P(("blk", "head"), None),
        P(("blk", "head"), None),
        P(),
        P("head"),
    )
    return jax.shard_map(
        per_device, mesh=mesh, in_specs=placed, out_specs=P("blk", "head"), check_vma=False
    )
```

```python
import functools
import math

import jax
import jax.numpy as jnp
from jax import lax
from jax.experimental import pallas as pl
from jax.experimental.pallas import tpu as pltpu
from jax.sharding import PartitionSpec as P

HD = 128
HEADS = 32
KV_HEADS = 8
WINDOW = 512
EPS = 1e-05
ORDER = sum(step << (3 * place) for place, step in enumerate((2, 6, 5, 3, 1, 7, 4, 0)))
MESH = pl.DeviceIdType.MESH


def kernel(
    nb, nh, chunk, halo, kv_heads, group,
    q_ref, k_ref, v_ref, seg_ref, o_ref, i_ref,
    kext, vext, qbuf, segbuf, bias, obuf, squares, inv,
    plus_send, plus_recv, minus_send, minus_recv, own_sem, seg_sem, o_send, o_recv,
    i_send, i_recv, near_sem, rounds_sem,
):
    b = lax.axis_index("blk")
    h = lax.axis_index("head")
    total_ranks = nb * nh
    rank = b * nh + h
    nxt = lax.rem(rank + 1, total_ranks)
    prv = lax.rem(rank + total_ranks - 1, total_ranks)
    nxt_b, nxt_h = lax.div(nxt, nh), lax.rem(nxt, nh)
    nxt_id = (nxt_b, nxt_h)
    prv_h = lax.rem(prv, nh)
    prv_id = (lax.div(prv, nh), prv_h)

    own_rows = pl.ds((halo - 1) * chunk, chunk)
    own_k = pltpu.make_async_copy(k_ref, kext.at[own_rows, :], own_sem.at[0])
    own_v = pltpu.make_async_copy(v_ref, vext.at[own_rows, :], own_sem.at[1])
    own_k.start()
    own_v.start()

    def seg_copy(m):
        row = jnp.maximum(nxt - halo + m, 0)
        return pltpu.make_async_copy(seg_ref.at[row], segbuf.at[m], seg_sem.at[m])

    for m in range(halo + 1):
        seg_copy(m).start()

    def rank_id(r):
        return (lax.div(r, nh), lax.rem(r, nh))

    def signal_both(sem, distance):
        for r in (rank + distance, rank + total_ranks - distance):
            pl.semaphore_signal(
                sem, inc=1, device_id=rank_id(lax.rem(r, total_ranks)), device_id_type=MESH
            )

    barrier = pltpu.get_barrier_semaphore()
    pl.semaphore_signal(barrier, inc=1, device_id=prv_id, device_id_type=MESH)
    pl.semaphore_wait(barrier, 1)
    pl.semaphore_signal(near_sem, inc=1, device_id=nxt_id, device_id_type=MESH)
    rounds = nh.bit_length() - 1

    def meet(j):
        pl.semaphore_wait(rounds_sem.at[j], 2)
        if j + 1 < rounds:
            signal_both(rounds_sem.at[j + 1], 2 << j)

    def pick(code, head):
        quad = lax.div(head, group)
        if kv_heads != 8:
            return lax.rem(quad + code, kv_heads), code + 1
        step = lax.rem(code, 8)
        flip = lax.rem(lax.div(quad, 4) + lax.div(step, 4), 2)
        return flip * 4 + lax.rem(quad + step, 4), lax.div(code, 8)

    start_code = ORDER if kv_heads == 8 else 0

    def cols(c, width):
        return pl.ds(pl.multiple_of(c * width, width), width)

    def plus_copy(hop, tensor, c):
        ext, own = (kext, k_ref) if tensor == 0 else (vext, v_ref)
        lanes = cols(c, HD)
        target = ext.at[pl.ds((halo - 2 - hop) * chunk, chunk), lanes]
        if hop == 0:
            source = own.at[:, lanes]
        else:
            source = ext.at[pl.ds((halo - 1 - hop) * chunk, chunk), lanes]
        return pltpu.make_async_remote_copy(
            src_ref=source, dst_ref=target,
            send_sem=plus_send.at[hop, tensor], recv_sem=plus_recv.at[hop, tensor, c],
            device_id=nxt_id, device_id_type=MESH,
        )

    def minus_copy(tensor, c):
        if tensor == 2:
            lanes = cols(c, group * HD)
            source, target = q_ref.at[:, lanes], qbuf.at[:, lanes]
        else:
            ext, own = (kext, k_ref) if tensor == 0 else (vext, v_ref)
            lanes = cols(c, HD)
            source, target = own.at[:, lanes], ext.at[pl.ds(halo * chunk, chunk), lanes]
        return pltpu.make_async_remote_copy(
            src_ref=source, dst_ref=target,
            send_sem=minus_send.at[tensor], recv_sem=minus_recv.at[tensor, c],
            device_id=prv_id, device_id_type=MESH,
        )

    def start_plus(s, code):
        c, code = pick(code, nxt_h)
        for tensor in range(2):
            plus_copy(0, tensor, c).start()
        return code

    def start_minus(s, code):
        c, code = pick(code, prv_h)
        for tensor in range(3):
            minus_copy(tensor, c).start()
        return code

    lax.fori_loop(0, kv_heads, start_plus, start_code)
    pl.semaphore_wait(near_sem, 1)
    lax.fori_loop(0, kv_heads, start_minus, start_code)
    signal_both(rounds_sem.at[0], 1)

    for m in range(halo + 1):
        seg_copy(m).wait()
    row_pos = lax.broadcasted_iota(jnp.int32, (chunk, chunk), 0)
    col_pos = lax.broadcasted_iota(jnp.int32, (chunk, chunk), 1)
    query_seg = jnp.transpose(jnp.broadcast_to(segbuf[halo], (chunk, chunk)))
    for m in range(halo + 1):
        key_seg = jnp.broadcast_to(segbuf[m], (chunk, chunk))
        col = col_pos + m * chunk
        allowed = (col > row_pos) & (col <= row_pos + WINDOW) & (key_seg == query_seg)
        allowed = allowed & ((nxt - halo + m) * chunk + col_pos >= 0)
        bias[:, m * chunk : (m + 1) * chunk] = jnp.where(allowed, 0.0, -1e30)

    meet(0)
    for hop in range(1, halo - 1):

        def forward(s, code):
            c, code = pick(code, nxt_h)
            for tensor in range(2):
                plus_copy(hop - 1, tensor, c).wait_recv()
                plus_copy(hop, tensor, c).start()
            return code

        lax.fori_loop(0, kv_heads, forward, start_code)
        if hop < rounds:
            meet(hop)

    own_k.wait()
    own_v.wait()
    for j in range(halo - 1, rounds):
        meet(j)
    squares[...] = jnp.zeros_like(squares)
    out_rows = pl.ds(pl.multiple_of(nxt_h * chunk, chunk), chunk)

    def send_head(g):
        stays = (nxt_b == b) & (g == h)

        @pl.when(stays)
        def _():
            pltpu.make_async_copy(obuf.at[g], o_ref.at[out_rows, :], o_recv).start()

        @pl.when(jnp.logical_not(stays))
        def _():
            pltpu.make_async_remote_copy(
                src_ref=obuf.at[g], dst_ref=o_ref.at[out_rows, :],
                send_sem=o_send, recv_sem=o_recv,
                device_id=(nxt_b, g), device_id_type=MESH,
            ).start()

    to_exponent = HD ** (-0.5) * math.log2(math.e)
    span = (halo + 1) * chunk

    def attend(s, code):
        c, code = pick(code, h)
        for tensor in range(2):
            plus_copy(halo - 2, tensor, c).wait_recv()
        for tensor in range(3):
            minus_copy(tensor, c).wait_recv()
        key = kext[:, cols(c, HD)]
        value = vext[:, cols(c, HD)]
        for first in range(0, group, 2):
            query = jnp.concatenate(
                [qbuf[:, cols(c * group + first + u, HD)] for u in range(2)], axis=0
            )
            scores = lax.dot_general(
                query, key, (((1,), (1,)), ((), ())), preferred_element_type=jnp.float32
            )
            scores = scores.reshape(2, chunk, span) + bias[...][None]
            rowmax = jnp.max(scores, axis=2, keepdims=True)
            prob = jnp.exp2((scores - rowmax) * to_exponent)
            total = jnp.sum(prob, axis=2, keepdims=True)
            weighted = jnp.dot(
                prob.astype(jnp.bfloat16).reshape(2 * chunk, span), value,
                preferred_element_type=jnp.float32,
            )
            out = (weighted.reshape(2, chunk, HD) / total).astype(jnp.bfloat16)
            obuf[pl.ds(c * group + first, 2)] = out
            wide = out.astype(jnp.float32)
            squares[...] += jnp.sum(wide * wide, axis=0)
            for u in range(2):
                send_head(c * group + first + u)
        return code

    lax.fori_loop(0, kv_heads, attend, start_code)

    width = nh * HD
    mean = jnp.sum(jnp.transpose(squares[...]), axis=0, keepdims=True) / width
    inv[...] = lax.rsqrt(mean + EPS)

    def send_inv(j, carry):
        g = lax.rem(h + 1 + j, nh)
        stays = (nxt_b == b) & (g == h)

        @pl.when(stays)
        def _():
            pltpu.make_async_copy(inv, i_ref.at[nxt_h], i_recv).start()

        @pl.when(jnp.logical_not(stays))
        def _():
            pltpu.make_async_remote_copy(
                src_ref=inv, dst_ref=i_ref.at[nxt_h], send_sem=i_send, recv_sem=i_recv,
                device_id=(nxt_b, g), device_id_type=MESH,
            ).start()

        return carry

    lax.fori_loop(0, nh, send_inv, 0)

    for hop in range(halo - 1):
        for tensor, ext in ((0, kext), (1, vext)):
            rows = ext.at[pl.ds(0, chunk), :]
            pltpu.make_async_copy(rows, rows, plus_send.at[hop, tensor]).wait()
    for tensor, ext in ((0, kext), (1, vext)):
        rows = ext.at[pl.ds(0, chunk), :]
        pltpu.make_async_copy(rows, rows, minus_send.at[tensor]).wait()
    pltpu.make_async_copy(qbuf, qbuf, minus_send.at[2]).wait()

    @pl.when(h == nh - 1)
    def _():
        pltpu.make_async_copy(obuf, obuf, o_send).wait()
        pltpu.make_async_copy(i_ref, i_ref, i_send).wait()

    @pl.when(h != nh - 1)
    def _():
        some = obuf.at[pl.ds(0, nh - 1)]
        pltpu.make_async_copy(some, some, o_send).wait()
        rows = i_ref.at[pl.ds(0, nh - 1)]
        pltpu.make_async_copy(rows, rows, i_send).wait()

    pltpu.make_async_copy(o_ref, o_ref, o_recv).wait()
    pltpu.make_async_copy(i_ref, i_ref, i_recv).wait()


def per_device(queries, keys, values, segments, norm_gain):
    nb, nh = lax.axis_size("blk"), lax.axis_size("head")
    chunk = queries.shape[0]
    halo = WINDOW // chunk
    kv_heads = keys.shape[1] // HD
    group = queries.shape[1] // keys.shape[1]
    any_spec = pl.BlockSpec(memory_space=pl.ANY)
    span = (halo + 1) * chunk
    attn, inv = pl.pallas_call(
        functools.partial(kernel, nb, nh, chunk, halo, kv_heads, group),
        out_shape=(
            jax.ShapeDtypeStruct((nh * chunk, HD), jnp.bfloat16),
            jax.ShapeDtypeStruct((nh, 1, chunk), jnp.float32),
        ),
        in_specs=[any_spec] * 4,
        out_specs=(any_spec, any_spec),
        scratch_shapes=[
            pltpu.VMEM((span, kv_heads * HD), jnp.bfloat16),
            pltpu.VMEM((span, kv_heads * HD), jnp.bfloat16),
            pltpu.VMEM((chunk, nh * HD), jnp.bfloat16),
            pltpu.VMEM((halo + 1, 1, chunk), jnp.int32),
            pltpu.VMEM((chunk, span), jnp.float32),
            pltpu.VMEM((nh, chunk, HD), jnp.bfloat16),
            pltpu.VMEM((chunk, HD), jnp.float32),
            pltpu.VMEM((1, chunk), jnp.float32),
            pltpu.SemaphoreType.DMA((halo - 1, 2)),
            pltpu.SemaphoreType.DMA((halo - 1, 2, kv_heads)),
            pltpu.SemaphoreType.DMA((3,)),
            pltpu.SemaphoreType.DMA((3, kv_heads)),
            pltpu.SemaphoreType.DMA((2,)),
            pltpu.SemaphoreType.DMA((halo + 1,)),
            pltpu.SemaphoreType.DMA,
            pltpu.SemaphoreType.DMA,
            pltpu.SemaphoreType.DMA,
            pltpu.SemaphoreType.DMA,
            pltpu.SemaphoreType.REGULAR,
            pltpu.SemaphoreType.REGULAR((nh.bit_length() - 1,)),
        ],
        compiler_params=pltpu.CompilerParams(
            collective_id=0, has_side_effects=True, vmem_limit_bytes=62 * 1024 * 1024
        ),
        name="attend_and_spread",
    )(queries, keys, values, segments.reshape(-1, 1, chunk))
    wide = attn.astype(jnp.float32)
    return (wide * norm_gain[None, :] * inv.reshape(-1, 1)).astype(jnp.bfloat16)


def solution(mesh):
    placed = (
        P(("blk", "head"), None),
        P(("blk", "head"), None),
        P(("blk", "head"), None),
        P(),
        P("head"),
    )
    return jax.shard_map(
        per_device, mesh=mesh, in_specs=placed, out_specs=P("blk", "head"), check_vma=False
    )
```

```python
import functools
import math

import jax
import jax.numpy as jnp
from jax import lax
from jax.experimental import pallas as pl
from jax.experimental.pallas import tpu as pltpu
from jax.sharding import PartitionSpec as P

HD = 128
HEADS = 32
KV_HEADS = 8
WINDOW = 512
EPS = 1e-05
ORDER = sum(step << (3 * place) for place, step in enumerate((2, 6, 5, 3, 1, 7, 4, 0)))
MESH = pl.DeviceIdType.MESH


def kernel(
    nb, nh, chunk, halo, kv_heads, group,
    q_ref, k_ref, v_ref, seg_ref, o_ref, i_ref,
    kext, vext, qbuf, segbuf, bias, obuf, squares, inv,
    plus_send, plus_recv, minus_send, minus_recv, own_sem, seg_sem, o_send, o_recv,
    i_send, i_recv, near_sem, rounds_sem,
):
    b = lax.axis_index("blk")
    h = lax.axis_index("head")
    total_ranks = nb * nh
    rank = b * nh + h
    nxt = lax.rem(rank + 1, total_ranks)
    prv = lax.rem(rank + total_ranks - 1, total_ranks)
    nxt_b, nxt_h = lax.div(nxt, nh), lax.rem(nxt, nh)
    nxt_id = (nxt_b, nxt_h)
    prv_h = lax.rem(prv, nh)
    prv_id = (lax.div(prv, nh), prv_h)

    own_rows = pl.ds((halo - 1) * chunk, chunk)
    own_k = pltpu.make_async_copy(k_ref, kext.at[own_rows, :], own_sem.at[0])
    own_v = pltpu.make_async_copy(v_ref, vext.at[own_rows, :], own_sem.at[1])
    own_k.start()
    own_v.start()

    def seg_copy(m):
        row = jnp.maximum(nxt - halo + m, 0)
        return pltpu.make_async_copy(seg_ref.at[row], segbuf.at[m], seg_sem.at[m])

    for m in range(halo + 1):
        seg_copy(m).start()

    def rank_id(r):
        return (lax.div(r, nh), lax.rem(r, nh))

    def signal_both(sem, distance):
        for r in (rank + distance, rank + total_ranks - distance):
            pl.semaphore_signal(
                sem, inc=1, device_id=rank_id(lax.rem(r, total_ranks)), device_id_type=MESH
            )

    barrier = pltpu.get_barrier_semaphore()
    pl.semaphore_signal(barrier, inc=1, device_id=prv_id, device_id_type=MESH)
    pl.semaphore_wait(barrier, 1)
    pl.semaphore_signal(near_sem, inc=1, device_id=nxt_id, device_id_type=MESH)
    rounds = nh.bit_length() - 1

    def meet(j):
        pl.semaphore_wait(rounds_sem.at[j], 2)
        if j + 1 < rounds:
            signal_both(rounds_sem.at[j + 1], 2 << j)

    def pick(code, head):
        quad = lax.div(head, group)
        if kv_heads != 8:
            return lax.rem(quad + code, kv_heads), code + 1
        step = lax.rem(code, 8)
        flip = lax.rem(lax.div(quad, 4) + lax.div(step, 4), 2)
        return flip * 4 + lax.rem(quad + step, 4), lax.div(code, 8)

    start_code = ORDER if kv_heads == 8 else 0

    def cols(c, width):
        return pl.ds(pl.multiple_of(c * width, width), width)

    def plus_copy(hop, tensor, c):
        ext, own = (kext, k_ref) if tensor == 0 else (vext, v_ref)
        lanes = cols(c, HD)
        target = ext.at[pl.ds((halo - 2 - hop) * chunk, chunk), lanes]
        if hop == 0:
            source = own.at[:, lanes]
        else:
            source = ext.at[pl.ds((halo - 1 - hop) * chunk, chunk), lanes]
        return pltpu.make_async_remote_copy(
            src_ref=source, dst_ref=target,
            send_sem=plus_send.at[hop, tensor], recv_sem=plus_recv.at[hop, tensor, c],
            device_id=nxt_id, device_id_type=MESH,
        )

    def minus_copy(tensor, c):
        if tensor == 2:
            lanes = cols(c, group * HD)
            source, target = q_ref.at[:, lanes], qbuf.at[:, lanes]
        else:
            ext, own = (kext, k_ref) if tensor == 0 else (vext, v_ref)
            lanes = cols(c, HD)
            source, target = own.at[:, lanes], ext.at[pl.ds(halo * chunk, chunk), lanes]
        return pltpu.make_async_remote_copy(
            src_ref=source, dst_ref=target,
            send_sem=minus_send.at[tensor], recv_sem=minus_recv.at[tensor, c],
            device_id=prv_id, device_id_type=MESH,
        )

    def start_plus(s, code):
        c, code = pick(code, nxt_h)
        for tensor in range(2):
            plus_copy(0, tensor, c).start()
        return code

    def start_minus(s, code):
        c, code = pick(code, prv_h)
        for tensor in range(3):
            minus_copy(tensor, c).start()
        return code

    lax.fori_loop(0, kv_heads, start_plus, start_code)
    pl.semaphore_wait(near_sem, 1)
    lax.fori_loop(0, kv_heads, start_minus, start_code)
    signal_both(rounds_sem.at[0], 1)

    for m in range(halo + 1):
        seg_copy(m).wait()
    row_pos = lax.broadcasted_iota(jnp.int32, (chunk, chunk), 0)
    col_pos = lax.broadcasted_iota(jnp.int32, (chunk, chunk), 1)
    query_seg = jnp.transpose(jnp.broadcast_to(segbuf[halo], (chunk, chunk)))
    for m in range(halo + 1):
        key_seg = jnp.broadcast_to(segbuf[m], (chunk, chunk))
        col = col_pos + m * chunk
        allowed = (col > row_pos) & (col <= row_pos + WINDOW) & (key_seg == query_seg)
        allowed = allowed & ((nxt - halo + m) * chunk + col_pos >= 0)
        bias[:, m * chunk : (m + 1) * chunk] = jnp.where(allowed, 0.0, -1e30)

    meet(0)
    for hop in range(1, halo - 1):

        def forward(s, code):
            c, code = pick(code, nxt_h)
            for tensor in range(2):
                plus_copy(hop - 1, tensor, c).wait_recv()
                plus_copy(hop, tensor, c).start()
            return code

        lax.fori_loop(0, kv_heads, forward, start_code)
        if hop < rounds:
            meet(hop)

    own_k.wait()
    own_v.wait()
    def last_rounds():
        for j in range(halo - 1, rounds):
            meet(j)

    for j in range(halo - 1, halo - 1):
        meet(j)
    squares[...] = jnp.zeros_like(squares)
    out_rows = pl.ds(pl.multiple_of(nxt_h * chunk, chunk), chunk)

    def send_head(g):
        stays = (nxt_b == b) & (g == h)

        @pl.when(stays)
        def _():
            pltpu.make_async_copy(obuf.at[g], o_ref.at[out_rows, :], o_recv).start()

        @pl.when(jnp.logical_not(stays))
        def _():
            pltpu.make_async_remote_copy(
                src_ref=obuf.at[g], dst_ref=o_ref.at[out_rows, :],
                send_sem=o_send, recv_sem=o_recv,
                device_id=(nxt_b, g), device_id_type=MESH,
            ).start()

    to_exponent = HD ** (-0.5) * math.log2(math.e)
    span = (halo + 1) * chunk

    def attend(s, code):
        c, code = pick(code, h)
        for tensor in range(2):
            plus_copy(halo - 2, tensor, c).wait_recv()
        for tensor in range(3):
            minus_copy(tensor, c).wait_recv()
        key = kext[:, cols(c, HD)]
        value = vext[:, cols(c, HD)]
        for first in range(0, group, 2):
            query = jnp.concatenate(
                [qbuf[:, cols(c * group + first + u, HD)] for u in range(2)], axis=0
            )
            scores = lax.dot_general(
                query, key, (((1,), (1,)), ((), ())), preferred_element_type=jnp.float32
            )
            scores = scores.reshape(2, chunk, span) + bias[...][None]
            rowmax = jnp.max(scores, axis=2, keepdims=True)
            prob = jnp.exp2((scores - rowmax) * to_exponent)
            total = jnp.sum(prob, axis=2, keepdims=True)
            weighted = jnp.dot(
                prob.astype(jnp.bfloat16).reshape(2 * chunk, span), value,
                preferred_element_type=jnp.float32,
            )
            out = (weighted.reshape(2, chunk, HD) / total).astype(jnp.bfloat16)
            obuf[pl.ds(c * group + first, 2)] = out
            wide = out.astype(jnp.float32)
            squares[...] += jnp.sum(wide * wide, axis=0)
            if first == 0:
                pl.when(s == 0)(last_rounds)
            for u in range(2):
                send_head(c * group + first + u)
        return code

    lax.fori_loop(0, kv_heads, attend, start_code)

    width = nh * HD
    mean = jnp.sum(jnp.transpose(squares[...]), axis=0, keepdims=True) / width
    inv[...] = lax.rsqrt(mean + EPS)

    def send_inv(j, carry):
        g = lax.rem(h + 1 + j, nh)
        stays = (nxt_b == b) & (g == h)

        @pl.when(stays)
        def _():
            pltpu.make_async_copy(inv, i_ref.at[nxt_h], i_recv).start()

        @pl.when(jnp.logical_not(stays))
        def _():
            pltpu.make_async_remote_copy(
                src_ref=inv, dst_ref=i_ref.at[nxt_h], send_sem=i_send, recv_sem=i_recv,
                device_id=(nxt_b, g), device_id_type=MESH,
            ).start()

        return carry

    lax.fori_loop(0, nh, send_inv, 0)

    for hop in range(halo - 1):
        for tensor, ext in ((0, kext), (1, vext)):
            rows = ext.at[pl.ds(0, chunk), :]
            pltpu.make_async_copy(rows, rows, plus_send.at[hop, tensor]).wait()
    for tensor, ext in ((0, kext), (1, vext)):
        rows = ext.at[pl.ds(0, chunk), :]
        pltpu.make_async_copy(rows, rows, minus_send.at[tensor]).wait()
    pltpu.make_async_copy(qbuf, qbuf, minus_send.at[2]).wait()

    @pl.when(h == nh - 1)
    def _():
        pltpu.make_async_copy(obuf, obuf, o_send).wait()
        pltpu.make_async_copy(i_ref, i_ref, i_send).wait()

    @pl.when(h != nh - 1)
    def _():
        some = obuf.at[pl.ds(0, nh - 1)]
        pltpu.make_async_copy(some, some, o_send).wait()
        rows = i_ref.at[pl.ds(0, nh - 1)]
        pltpu.make_async_copy(rows, rows, i_send).wait()

    pltpu.make_async_copy(o_ref, o_ref, o_recv).wait()
    pltpu.make_async_copy(i_ref, i_ref, i_recv).wait()


def per_device(queries, keys, values, segments, norm_gain):
    nb, nh = lax.axis_size("blk"), lax.axis_size("head")
    chunk = queries.shape[0]
    halo = WINDOW // chunk
    kv_heads = keys.shape[1] // HD
    group = queries.shape[1] // keys.shape[1]
    any_spec = pl.BlockSpec(memory_space=pl.ANY)
    span = (halo + 1) * chunk
    attn, inv = pl.pallas_call(
        functools.partial(kernel, nb, nh, chunk, halo, kv_heads, group),
        out_shape=(
            jax.ShapeDtypeStruct((nh * chunk, HD), jnp.bfloat16),
            jax.ShapeDtypeStruct((nh, 1, chunk), jnp.float32),
        ),
        in_specs=[any_spec] * 4,
        out_specs=(any_spec, any_spec),
        scratch_shapes=[
            pltpu.VMEM((span, kv_heads * HD), jnp.bfloat16),
            pltpu.VMEM((span, kv_heads * HD), jnp.bfloat16),
            pltpu.VMEM((chunk, nh * HD), jnp.bfloat16),
            pltpu.VMEM((halo + 1, 1, chunk), jnp.int32),
            pltpu.VMEM((chunk, span), jnp.float32),
            pltpu.VMEM((nh, chunk, HD), jnp.bfloat16),
            pltpu.VMEM((chunk, HD), jnp.float32),
            pltpu.VMEM((1, chunk), jnp.float32),
            pltpu.SemaphoreType.DMA((halo - 1, 2)),
            pltpu.SemaphoreType.DMA((halo - 1, 2, kv_heads)),
            pltpu.SemaphoreType.DMA((3,)),
            pltpu.SemaphoreType.DMA((3, kv_heads)),
            pltpu.SemaphoreType.DMA((2,)),
            pltpu.SemaphoreType.DMA((halo + 1,)),
            pltpu.SemaphoreType.DMA,
            pltpu.SemaphoreType.DMA,
            pltpu.SemaphoreType.DMA,
            pltpu.SemaphoreType.DMA,
            pltpu.SemaphoreType.REGULAR,
            pltpu.SemaphoreType.REGULAR((nh.bit_length() - 1,)),
        ],
        compiler_params=pltpu.CompilerParams(
            collective_id=0, has_side_effects=True, vmem_limit_bytes=62 * 1024 * 1024
        ),
        name="attend_and_spread",
    )(queries, keys, values, segments.reshape(-1, 1, chunk))
    wide = attn.astype(jnp.float32)
    return (wide * norm_gain[None, :] * inv.reshape(-1, 1)).astype(jnp.bfloat16)


def solution(mesh):
    placed = (
        P(("blk", "head"), None),
        P(("blk", "head"), None),
        P(("blk", "head"), None),
        P(),
        P("head"),
    )
    return jax.shard_map(
        per_device, mesh=mesh, in_specs=placed, out_specs=P("blk", "head"), check_vma=False
    )
```

```python
import functools
import math

import jax
import jax.numpy as jnp
from jax import lax
from jax.experimental import pallas as pl
from jax.experimental.pallas import tpu as pltpu
from jax.sharding import PartitionSpec as P

HD = 128
HEADS = 32
KV_HEADS = 8
WINDOW = 512
EPS = 1e-05
ORDER = sum(step << (3 * place) for place, step in enumerate((2, 6, 5, 3, 1, 7, 4, 0)))
MESH = pl.DeviceIdType.MESH


def kernel(
    nb, nh, chunk, halo, kv_heads, group,
    q_ref, k_ref, v_ref, seg_ref, o_ref, i_ref,
    kext, vext, qbuf, segbuf, bias, obuf, squares, inv,
    plus_send, plus_recv, minus_send, minus_recv, own_sem, seg_sem, o_send, o_recv,
    i_send, i_recv, near_sem, rounds_sem,
):
    b = lax.axis_index("blk")
    h = lax.axis_index("head")
    total_ranks = nb * nh
    rank = b * nh + h
    nxt = lax.rem(rank + 1, total_ranks)
    prv = lax.rem(rank + total_ranks - 1, total_ranks)
    nxt_b, nxt_h = lax.div(nxt, nh), lax.rem(nxt, nh)
    nxt_id = (nxt_b, nxt_h)
    prv_h = lax.rem(prv, nh)
    prv_id = (lax.div(prv, nh), prv_h)

    own_rows = pl.ds((halo - 1) * chunk, chunk)
    own_k = pltpu.make_async_copy(k_ref, kext.at[own_rows, :], own_sem.at[0])
    own_v = pltpu.make_async_copy(v_ref, vext.at[own_rows, :], own_sem.at[1])
    own_k.start()
    own_v.start()

    def seg_copy(m):
        row = jnp.maximum(nxt - halo + m, 0)
        return pltpu.make_async_copy(seg_ref.at[row], segbuf.at[m], seg_sem.at[m])

    for m in range(halo + 1):
        seg_copy(m).start()

    def rank_id(r):
        return (lax.div(r, nh), lax.rem(r, nh))

    def signal_both(sem, distance):
        for r in (rank + distance, rank + total_ranks - distance):
            pl.semaphore_signal(
                sem, inc=1, device_id=rank_id(lax.rem(r, total_ranks)), device_id_type=MESH
            )

    barrier = pltpu.get_barrier_semaphore()
    pl.semaphore_signal(barrier, inc=1, device_id=prv_id, device_id_type=MESH)
    pl.semaphore_wait(barrier, 1)
    pl.semaphore_signal(near_sem, inc=1, device_id=nxt_id, device_id_type=MESH)
    rounds = nh.bit_length() - 1

    def meet(j):
        pl.semaphore_wait(rounds_sem.at[j], 2)
        if j + 1 < rounds:
            signal_both(rounds_sem.at[j + 1], 2 << j)

    def pick(code, head):
        quad = lax.div(head, group)
        if kv_heads != 8:
            return lax.rem(quad + code, kv_heads), code + 1
        step = lax.rem(code, 8)
        flip = lax.rem(lax.div(quad, 4) + lax.div(step, 4), 2)
        return flip * 4 + lax.rem(quad + step, 4), lax.div(code, 8)

    start_code = ORDER if kv_heads == 8 else 0

    def cols(c, width):
        return pl.ds(pl.multiple_of(c * width, width), width)

    def plus_copy(hop, tensor, c):
        ext, own = (kext, k_ref) if tensor == 0 else (vext, v_ref)
        lanes = cols(c, HD)
        target = ext.at[pl.ds((halo - 2 - hop) * chunk, chunk), lanes]
        if hop == 0:
            source = own.at[:, lanes]
        else:
            source = ext.at[pl.ds((halo - 1 - hop) * chunk, chunk), lanes]
        return pltpu.make_async_remote_copy(
            src_ref=source, dst_ref=target,
            send_sem=plus_send.at[hop, tensor], recv_sem=plus_recv.at[hop, tensor, c],
            device_id=nxt_id, device_id_type=MESH,
        )

    def minus_copy(tensor, c):
        if tensor == 2:
            lanes = cols(c, group * HD)
            source, target = q_ref.at[:, lanes], qbuf.at[:, lanes]
        else:
            ext, own = (kext, k_ref) if tensor == 0 else (vext, v_ref)
            lanes = cols(c, HD)
            source, target = own.at[:, lanes], ext.at[pl.ds(halo * chunk, chunk), lanes]
        return pltpu.make_async_remote_copy(
            src_ref=source, dst_ref=target,
            send_sem=minus_send.at[tensor], recv_sem=minus_recv.at[tensor, c],
            device_id=prv_id, device_id_type=MESH,
        )

    def start_plus(s, code):
        c, code = pick(code, nxt_h)
        for tensor in range(2):
            plus_copy(0, tensor, c).start()
        return code

    def start_minus(s, code):
        c, code = pick(code, prv_h)
        for tensor in range(3):
            minus_copy(tensor, c).start()
        return code

    lax.fori_loop(0, kv_heads, start_plus, start_code)
    pl.semaphore_wait(near_sem, 1)
    lax.fori_loop(0, kv_heads, start_minus, start_code)
    signal_both(rounds_sem.at[0], 1)

    for m in range(halo + 1):
        seg_copy(m).wait()
    row_pos = lax.broadcasted_iota(jnp.int32, (chunk, chunk), 0)
    col_pos = lax.broadcasted_iota(jnp.int32, (chunk, chunk), 1)
    query_seg = jnp.transpose(jnp.broadcast_to(segbuf[halo], (chunk, chunk)))
    for m in range(halo + 1):
        key_seg = jnp.broadcast_to(segbuf[m], (chunk, chunk))
        col = col_pos + m * chunk
        allowed = (col > row_pos) & (col <= row_pos + WINDOW) & (key_seg == query_seg)
        allowed = allowed & ((nxt - halo + m) * chunk + col_pos >= 0)
        bias[:, m * chunk : (m + 1) * chunk] = jnp.where(allowed, 0.0, -1e30)

    meet(0)
    for hop in range(1, halo - 1):

        def forward(s, code):
            c, code = pick(code, nxt_h)
            for tensor in range(2):
                plus_copy(hop - 1, tensor, c).wait_recv()
                plus_copy(hop, tensor, c).start()
            return code

        lax.fori_loop(0, kv_heads, forward, start_code)
        if hop < rounds:
            meet(hop)

    own_k.wait()
    own_v.wait()
    def last_rounds():
        for j in range(halo - 1, rounds):
            meet(j)

    for j in range(halo - 1, halo - 1):
        meet(j)
    squares[...] = jnp.zeros_like(squares)
    out_rows = pl.ds(pl.multiple_of(nxt_h * chunk, chunk), chunk)

    def send_head(g):
        stays = (nxt_b == b) & (g == h)

        @pl.when(stays)
        def _():
            pltpu.make_async_copy(obuf.at[g], o_ref.at[out_rows, :], o_recv).start()

        @pl.when(jnp.logical_not(stays))
        def _():
            pltpu.make_async_remote_copy(
                src_ref=obuf.at[g], dst_ref=o_ref.at[out_rows, :],
                send_sem=o_send, recv_sem=o_recv,
                device_id=(nxt_b, g), device_id_type=MESH,
            ).start()

    to_exponent = HD ** (-0.5) * math.log2(math.e)
    span = (halo + 1) * chunk

    def attend(s, code):
        c, code = pick(code, h)
        for tensor in range(2):
            plus_copy(halo - 2, tensor, c).wait_recv()
        for tensor in range(3):
            minus_copy(tensor, c).wait_recv()
        key = kext[:, cols(c, HD)]
        value = vext[:, cols(c, HD)]
        for first in range(0, group, 2):
            query = jnp.concatenate(
                [qbuf[:, cols(c * group + first + u, HD)] for u in range(2)], axis=0
            )
            scores = lax.dot_general(
                query, key, (((1,), (1,)), ((), ())), preferred_element_type=jnp.float32
            )
            scores = scores.reshape(2, chunk, span) + bias[...][None]
            rowmax = jnp.max(scores, axis=2, keepdims=True)
            prob = jnp.exp2((scores - rowmax) * to_exponent)
            total = jnp.sum(prob, axis=2, keepdims=True)
            weighted = jnp.dot(
                prob.astype(jnp.bfloat16).reshape(2 * chunk, span), value,
                preferred_element_type=jnp.float32,
            )
            out = (weighted.reshape(2, chunk, HD) * (1.0 / total)).astype(jnp.bfloat16)
            obuf[pl.ds(c * group + first, 2)] = out
            wide = out.astype(jnp.float32)
            squares[...] += jnp.sum(wide * wide, axis=0)
            if first == 0:
                pl.when(s == 0)(last_rounds)
            for u in range(2):
                send_head(c * group + first + u)
        return code

    lax.fori_loop(0, kv_heads, attend, start_code)

    width = nh * HD
    mean = jnp.sum(jnp.transpose(squares[...]), axis=0, keepdims=True) / width
    inv[...] = lax.rsqrt(mean + EPS)

    def send_inv(j, carry):
        g = lax.rem(h + 1 + j, nh)
        stays = (nxt_b == b) & (g == h)

        @pl.when(stays)
        def _():
            pltpu.make_async_copy(inv, i_ref.at[nxt_h], i_recv).start()

        @pl.when(jnp.logical_not(stays))
        def _():
            pltpu.make_async_remote_copy(
                src_ref=inv, dst_ref=i_ref.at[nxt_h], send_sem=i_send, recv_sem=i_recv,
                device_id=(nxt_b, g), device_id_type=MESH,
            ).start()

        return carry

    lax.fori_loop(0, nh, send_inv, 0)

    for hop in range(halo - 1):
        for tensor, ext in ((0, kext), (1, vext)):
            rows = ext.at[pl.ds(0, chunk), :]
            pltpu.make_async_copy(rows, rows, plus_send.at[hop, tensor]).wait()
    for tensor, ext in ((0, kext), (1, vext)):
        rows = ext.at[pl.ds(0, chunk), :]
        pltpu.make_async_copy(rows, rows, minus_send.at[tensor]).wait()
    pltpu.make_async_copy(qbuf, qbuf, minus_send.at[2]).wait()

    @pl.when(h == nh - 1)
    def _():
        pltpu.make_async_copy(obuf, obuf, o_send).wait()
        pltpu.make_async_copy(i_ref, i_ref, i_send).wait()

    @pl.when(h != nh - 1)
    def _():
        some = obuf.at[pl.ds(0, nh - 1)]
        pltpu.make_async_copy(some, some, o_send).wait()
        rows = i_ref.at[pl.ds(0, nh - 1)]
        pltpu.make_async_copy(rows, rows, i_send).wait()

    pltpu.make_async_copy(o_ref, o_ref, o_recv).wait()
    pltpu.make_async_copy(i_ref, i_ref, i_recv).wait()


def per_device(queries, keys, values, segments, norm_gain):
    nb, nh = lax.axis_size("blk"), lax.axis_size("head")
    chunk = queries.shape[0]
    halo = WINDOW // chunk
    kv_heads = keys.shape[1] // HD
    group = queries.shape[1] // keys.shape[1]
    any_spec = pl.BlockSpec(memory_space=pl.ANY)
    span = (halo + 1) * chunk
    attn, inv = pl.pallas_call(
        functools.partial(kernel, nb, nh, chunk, halo, kv_heads, group),
        out_shape=(
            jax.ShapeDtypeStruct((nh * chunk, HD), jnp.bfloat16),
            jax.ShapeDtypeStruct((nh, 1, chunk), jnp.float32),
        ),
        in_specs=[any_spec] * 4,
        out_specs=(any_spec, any_spec),
        scratch_shapes=[
            pltpu.VMEM((span, kv_heads * HD), jnp.bfloat16),
            pltpu.VMEM((span, kv_heads * HD), jnp.bfloat16),
            pltpu.VMEM((chunk, nh * HD), jnp.bfloat16),
            pltpu.VMEM((halo + 1, 1, chunk), jnp.int32),
            pltpu.VMEM((chunk, span), jnp.float32),
            pltpu.VMEM((nh, chunk, HD), jnp.bfloat16),
            pltpu.VMEM((chunk, HD), jnp.float32),
            pltpu.VMEM((1, chunk), jnp.float32),
            pltpu.SemaphoreType.DMA((halo - 1, 2)),
            pltpu.SemaphoreType.DMA((halo - 1, 2, kv_heads)),
            pltpu.SemaphoreType.DMA((3,)),
            pltpu.SemaphoreType.DMA((3, kv_heads)),
            pltpu.SemaphoreType.DMA((2,)),
            pltpu.SemaphoreType.DMA((halo + 1,)),
            pltpu.SemaphoreType.DMA,
            pltpu.SemaphoreType.DMA,
            pltpu.SemaphoreType.DMA,
            pltpu.SemaphoreType.DMA,
            pltpu.SemaphoreType.REGULAR,
            pltpu.SemaphoreType.REGULAR((nh.bit_length() - 1,)),
        ],
        compiler_params=pltpu.CompilerParams(
            collective_id=0, has_side_effects=True, vmem_limit_bytes=62 * 1024 * 1024
        ),
        name="attend_and_spread",
    )(queries, keys, values, segments.reshape(-1, 1, chunk))
    wide = attn.astype(jnp.float32)
    return (wide * norm_gain[None, :] * inv.reshape(-1, 1)).astype(jnp.bfloat16)


def solution(mesh):
    placed = (
        P(("blk", "head"), None),
        P(("blk", "head"), None),
        P(("blk", "head"), None),
        P(),
        P("head"),
    )
    return jax.shard_map(
        per_device, mesh=mesh, in_specs=placed, out_specs=P("blk", "head"), check_vma=False
    )
```
